32 devices in a mesh: groups: 1, ex: 32 (over z, y, x, core).
Axes of the slice: x: 2, y: 2, z: 4, core: 2. Of those that a mesh axis runs over, the one named last changes fastest.
Arguments:
- residual_in: bfloat16 [2, 1024, 2048], P(None, ('groups', 'ex')), may hold values from -6 to 6
- queries: bfloat16 [2, 1024, 2048], P(None, ('groups', 'ex')), may hold values from -100 to 100
- new_entries: bfloat16 [2, 1024, 2, 256], P(None, ('groups', 'ex')), may hold values from -6 to 6
- cache_keys: bfloat16 [2, 1024, 64, 256], P(None, ('groups', 'ex')), may hold values from -4.5 to 4.5
- cache_values: bfloat16 [2, 1024, 64, 256], P(None, ('groups', 'ex')), may hold values from -6 to 6
- lengths: int32 [2, 1024], P(None, ('groups', 'ex')), may hold values from 2 to 64, as said below
- skip_flags: int32 [2, 1024], P(None, ('groups', 'ex')), may hold values 0 or 1
- expert_ids: int32 [2, 1024, 8], P(None, ('groups', 'ex')), may hold values from 0 to 31, all different within a row; in each aligned block of 32 rows (0 to 31, 32 to 63, ..., all dimensions but the last counted through in order) at most 16 rows name the same one
- gate_weights: float32 [2, 1024, 8], P(None, ('groups', 'ex')), may hold values from 0.1 to 1
- norm_gain: float32 [2048], replicated, may hold values from 0.1 to 1.9
- gate_proj: bfloat16 [32, 2048, 768], P('ex'), may hold values from -0.125 to 0.125
- up_proj: bfloat16 [32, 2048, 768], P('ex'), may hold values from -0.125 to 0.125
- down_proj: bfloat16 [32, 768, 2048], P('ex'), may hold values from -0.21875 to 0.21875
Outputs:
- layer_out: bfloat16 [2, 1024, 2048], P(None, ('groups', 'ex'))
The draws below stay inside these ranges and needn't reach their ends.
Inputs may be any that keep to these rules, and one draw needn't show every extreme that they name: `expert_ids`: in each micro-batch, the 32 rows of one device name any one expert at most 16 times; each row names 8 different experts. `lengths`: in each micro-batch, every device's block of 32 rows holds a row of length 64.
All inputs are finite; a program needn't handle non-finite values. No bound on the sum of `skip_flags` on one device may be relied on, other than what follows from the above.
Results may differ from the reference program's by a relative error of at most 0.0065.
Values may be sent and summed in bfloat16 or wider, within the bound.
A program may use at most 128 MiB of HBM per device.

```python
import math
import jax
import jax.numpy as jnp
import numpy as np
from jax import lax

D = 2048
FF = 768
HEADS = 16
KEY_VALUE_HEADS = 2
HEAD_WIDTH = 128
TOPK = 8
MICRO = 2
ROWS_DEV = 32
CACHE = 64
EXPERTS = 32
TOKENS = 1024
CAP = 16
N_EX = 32


def attention_pair(key):
    key_keys = jax.random.fold_in(key, 11)
    key_query = jax.random.fold_in(key, 12)
    keys = jax.random.truncated_normal(key_keys, -4.5, 4.5, (MICRO, TOKENS, CACHE, KEY_VALUE_HEADS * HEAD_WIDTH), jnp.float32)
    query = jax.random.truncated_normal(key_query, -4.5, 4.5, (MICRO, TOKENS, HEADS * HEAD_WIDTH), jnp.float32)
    return (keys, query)


def draw_cache_keys(key, part):
    keys, query = attention_pair(key)
    return keys.astype(jnp.bfloat16)


def draw_queries(key, part):
    keys, query = attention_pair(key)
    return query.astype(jnp.bfloat16)


def draw_lengths(key, part):
    key_a = jax.random.fold_in(key, 21)
    key_b = jax.random.fold_in(key, 22)
    key_c = jax.random.fold_in(key, 23)
    first = jax.random.randint(key_a, (MICRO, TOKENS), 0, CACHE - 1)
    second = jax.random.randint(key_b, (MICRO, TOKENS), 0, CACHE - 1)
    lens = 2 + first * second // (CACHE - 2)
    lens = lens.reshape(MICRO, TOKENS // ROWS_DEV, ROWS_DEV)
    where_full = jax.random.randint(key_c, (MICRO, TOKENS // ROWS_DEV, 1), 0, ROWS_DEV)
    position = jnp.arange(ROWS_DEV, dtype=jnp.int32)[None, None, :]
    lens = jnp.where(position == where_full, CACHE, lens)
    return lens.reshape(MICRO, TOKENS).astype(jnp.int32)


def place_ends(values, rng, smallest, largest):
    dims = values.shape
    spot = [jax.random.randint(jax.random.fold_in(rng, axis), (), 0, dims[axis]) for axis in range(len(dims))]
    values = values.at[tuple(spot)].set(smallest)
    longest = dims.index(max(dims))
    spot[longest] = (spot[longest] + 1) % dims[longest]
    return values.at[tuple(spot)].set(largest)


def shard_levels(rng, extent, shards, low, largest):
    factor_of, own = 1.0, jax.random.fold_in(rng, 6)
    for dim, parts in shards:
        heights = jnp.exp(jax.random.uniform(jax.random.fold_in(own, dim), (parts,), jnp.float32, low / len(shards), largest / len(shards)))
        factor_of = factor_of * jnp.repeat(heights, extent[dim] // parts).reshape([-1 if axis == dim else 1 for axis in range(len(extent))])
    return factor_of


def routed_block(key, own, number, rows, amount, top, reach, lean):
    ranking = jax.random.permutation(key, amount)
    heavy_load, usual = portions_of(amount, rows * top, reach, lean, True), portions_of(amount, rows * top, reach, lean, False)
    places = jnp.arange(amount)

    def named(sizes, rotation):
        used = int((sizes > 0).sum())
        fixed = max(1, used // 4)
        moved = fixed + (places - fixed + rotation * (used - fixed)) % max(1, amount - fixed)
        return jnp.zeros((amount,), jnp.int32).at[ranking[jnp.where(places < fixed, places, moved)]].set(jnp.asarray(sizes, jnp.int32))

    sizes = jnp.where(number % 4 == 0, named(heavy_load, number // 4), named(usual, number - number // 4 - 1))
    mixed = jax.random.permutation(jax.random.fold_in(own, 3), amount)
    giver, taker = mixed[0:amount // 2 * 2:2], mixed[1:amount // 2 * 2:2]
    slack = jnp.minimum(sizes[giver] - 1, reach - sizes[taker]) // 2
    slack = jnp.where((giver == ranking[0]) | (taker == ranking[0]) | (sizes[taker] == 0), 0, jnp.maximum(slack, 0))
    moved = jax.random.randint(jax.random.fold_in(own, 4), (amount // 2,), 0, 1 << 20) % (slack + 1)
    sizes = sizes.at[giver].add(-moved).at[taker].add(moved)
    labels = jnp.searchsorted(jnp.cumsum(sizes), jnp.arange(rows * top), side="right").astype(jnp.int32)
    grid = labels.reshape(top, rows).T
    grid = grid[jax.random.permutation(jax.random.fold_in(own, 1), rows)]
    rotation = jax.random.randint(jax.random.fold_in(own, 2), (rows, 1), 0, top)
    return jnp.take_along_axis(grid, (jnp.arange(top)[None, :] + rotation) % top, axis=1)


def portions_of(count, total, bound, skew, full):
    loads = [(1 << 20) // math.isqrt(rank ** skew) + 1 for rank in range(1, count + 1)]
    largest = bound if full else min(bound, max(-(-total // count), total * loads[0] // sum(loads)))
    least = 1 if total - largest >= count - 1 else 0
    counts, rest = [largest] + [least] * (count - 1), total - largest - least * (count - 1)
    while rest > 0:
        candidates = [i for i in range(1, count) if counts[i] < largest] or [i for i in range(1, count) if counts[i] < bound]
        pool, budget = sum([loads[i] for i in candidates]), rest
        for i in candidates:
            extra = min(bound - counts[i], max(1, budget * loads[i] // pool), rest)
            counts[i] = counts[i] + extra
            rest = rest - extra
    return np.array(counts)


def bell_draw(key, dims, deviation, reach, pieces=(), kind=jnp.bfloat16):
    level = shard_levels(key, dims, pieces, -0.22, 0.18) if pieces else 1.0
    values = jax.random.normal(key, dims, jnp.float32) * deviation * level
    return jnp.minimum(jnp.maximum(values, -reach), reach).astype(kind)


def setup_inputs(seed: int = 0, part: int = 0) -> dict:
    key_list = jax.random.split(jax.random.key(seed), 14)
    own_keys = jax.random.split(jax.random.fold_in(key_list[13], part), 14)
    residual_in = bell_draw(own_keys[0], (MICRO, TOKENS, D), 1.0, 6.0, ((1, 32),))
    queries = draw_queries(jax.random.fold_in(jax.random.fold_in(key_list[13], part), 71), part)
    new_entries = bell_draw(own_keys[2], (MICRO, TOKENS, 2, KEY_VALUE_HEADS * HEAD_WIDTH), 1.0, 6.0, ((1, 32),))
    cache_keys = draw_cache_keys(jax.random.fold_in(jax.random.fold_in(key_list[13], part), 71), part)
    cache_values = bell_draw(own_keys[4], (MICRO, TOKENS, CACHE, KEY_VALUE_HEADS * HEAD_WIDTH), 1.0, 6.0, ((1, 32),))
    lengths = draw_lengths(jax.random.fold_in(jax.random.fold_in(key_list[13], part), 71), part)
    skip_flags = place_ends((jax.random.randint(own_keys[6], (MICRO, TOKENS), 0, 8) < 1).astype(jnp.int32), jax.random.fold_in(own_keys[6], 1), 0, 1)
    expert_ids_keys = jax.random.split(jax.random.fold_in(own_keys[7], 1), MICRO * TOKENS // ROWS_DEV)
    expert_ids_turns = jax.random.permutation(jax.random.fold_in(own_keys[7], 3), MICRO * TOKENS // ROWS_DEV)
    expert_ids = jax.vmap(lambda own, number: routed_block(jax.random.fold_in(own_keys[7], 2), own, number, ROWS_DEV, EXPERTS, TOPK, CAP, 2))(expert_ids_keys, expert_ids_turns).reshape((MICRO, TOKENS, TOPK))
    gate_weights = jnp.clip(jnp.exp(math.log(1.0) - 2.3025851 * jax.random.uniform(own_keys[8], (MICRO, TOKENS, TOPK), jnp.float32) ** shard_levels(own_keys[8], (MICRO, TOKENS, TOPK), ((1, 32),), -0.2, 0.2)), 0.1, 1.0)
    norm_gain = jnp.clip(1.0 + 0.18 * jax.random.normal(key_list[9], (D,), jnp.float32), 0.1, 1.9)
    gate_proj = bell_draw(key_list[10], (EXPERTS, D, FF), D ** -0.5, 0.125, ((0, 32),))
    up_proj = bell_draw(key_list[11], (EXPERTS, D, FF), D ** -0.5, 0.125, ((0, 32),))
    down_proj = bell_draw(key_list[12], (EXPERTS, FF, D), FF ** -0.5, 0.21875, ((0, 32),))
    return {"residual_in": residual_in, "queries": queries, "new_entries": new_entries, "cache_keys": cache_keys, "cache_values": cache_values, "lengths": lengths, "skip_flags": skip_flags, "expert_ids": expert_ids, "gate_weights": gate_weights, "norm_gain": norm_gain, "gate_proj": gate_proj, "up_proj": up_proj, "down_proj": down_proj}


def attend(queries, entries, keys, value_entries, lengths):
    token_row_count = queries.shape[0]
    cache_slot_index = keys.shape[1]
    group = HEADS // KEY_VALUE_HEADS
    scale = HEAD_WIDTH ** (-0.5)
    qvec = queries.reshape(token_row_count, KEY_VALUE_HEADS, group, HEAD_WIDTH).astype(jnp.float32)
    kmat = keys.reshape(token_row_count, cache_slot_index, KEY_VALUE_HEADS, HEAD_WIDTH).astype(jnp.float32)
    value_matrix = value_entries.reshape(token_row_count, cache_slot_index, KEY_VALUE_HEADS, HEAD_WIDTH).astype(jnp.float32)
    own_key = entries[:, 0].reshape(token_row_count, KEY_VALUE_HEADS, HEAD_WIDTH).astype(jnp.float32)
    self_value_vector = entries[:, 1].reshape(token_row_count, KEY_VALUE_HEADS, HEAD_WIDTH).astype(jnp.float32)
    cache_scores = jnp.einsum('rkgd,rlkd->rkgl', qvec, kmat) * scale
    own_scores = jnp.einsum('rkgd,rkd->rkg', qvec, own_key) * scale
    live = (jnp.arange(cache_slot_index, dtype=jnp.int32)[None, :] < lengths[:, None])[:, None, None, :]
    cache_scores = jnp.where(live, cache_scores, -1e+30)
    top = jnp.maximum(lax.optimization_barrier(jnp.max(cache_scores, axis=-1)), own_scores)
    cache_p = jnp.where(live, jnp.exp(cache_scores - top[..., None]), 0.0)
    own_p = jnp.exp(own_scores - top)
    total = lax.optimization_barrier(jnp.sum(cache_p, axis=-1)) + own_p
    cache_weight_part = (cache_p / total[..., None]).astype(jnp.bfloat16).astype(jnp.float32)
    self_weight_part = (own_p / total).astype(jnp.bfloat16).astype(jnp.float32)
    blended_output = jnp.einsum('xtio,xotw->xtiw', cache_weight_part, value_matrix) + self_weight_part[..., None] * self_value_vector[:, :, None, :]
    return blended_output.reshape(token_row_count, HEADS * HEAD_WIDTH).astype(jnp.bfloat16)

def expert_apply(inputs):
    rows_in, w_gate, w_up, w_down = inputs
    flat = rows_in.reshape(-1, D)
    gate = jnp.dot(flat, w_gate, preferred_element_type=jnp.float32)
    upper = jnp.dot(flat, w_up, preferred_element_type=jnp.float32)
    hidden = (jax.nn.silu(gate) * upper).astype(jnp.bfloat16)
    result = jnp.dot(hidden, w_down, preferred_element_type=jnp.float32).astype(jnp.bfloat16)
    return result.reshape(rows_in.shape)

def reference(residual_in, queries, new_entries, cache_keys, cache_values, lengths, skip_flags, expert_ids, gate_weights, norm_gain, gate_proj, up_proj, down_proj):
    results = []
    for micro in range(MICRO):
        attended = attend(queries[micro], new_entries[micro], cache_keys[micro], cache_values[micro], lengths[micro])
        stream = residual_in[micro].astype(jnp.float32) + attended.astype(jnp.float32)
        meansq = lax.optimization_barrier(jnp.mean(stream * stream, axis=-1, keepdims=True))
        normed = (stream / jnp.sqrt(meansq + 1e-06) * norm_gain[None, :]).astype(jnp.bfloat16)
        blocks = expert_ids[micro].reshape(N_EX, ROWS_DEV * TOPK)
        onehot = (blocks[:, :, None] == jnp.arange(EXPERTS, dtype=jnp.int32)[None, None, :]).astype(jnp.int32)
        before = jnp.cumsum(onehot, axis=1) - onehot
        rank = lax.optimization_barrier(jnp.sum(before * onehot, axis=-1)).reshape(-1).astype(jnp.int32)
        ids_flat = blocks.reshape(-1).astype(jnp.int32)
        row_flat = jnp.repeat(jnp.arange(TOKENS, dtype=jnp.int32), TOPK)
        src_flat = (row_flat // ROWS_DEV).astype(jnp.int32)
        buffer = jnp.zeros((EXPERTS, N_EX, CAP, D), normed.dtype)
        buffer = buffer.at[ids_flat, src_flat, rank].set(normed[row_flat])
        outputs = lax.map(expert_apply, (buffer, gate_proj, up_proj, down_proj))
        picked = outputs[ids_flat, src_flat, rank].reshape(TOKENS, TOPK, D).astype(jnp.float32)
        gates = gate_weights[micro]
        gates = gates / lax.optimization_barrier(jnp.sum(gates, axis=-1, keepdims=True))
        mixture = lax.optimization_barrier(jnp.sum(gates[:, :, None] * picked, axis=1))
        merged = (stream + mixture).astype(jnp.bfloat16)
        results.append(jnp.where(skip_flags[micro][:, None] == 1, residual_in[micro], merged))
    return jnp.stack(results, axis=0)
```

```python
import jax
import jax.numpy as jnp
from jax import lax
from jax.sharding import PartitionSpec as P

HEADS = 16
KEY_VALUE_HEADS = 2
HEAD_WIDTH = 128


def attend(queries, entries, keys, value_entries, lengths):
    token_row_count = queries.shape[0]
    cache_slot_index = keys.shape[1]
    group = HEADS // KEY_VALUE_HEADS
    scale = HEAD_WIDTH ** (-0.5)
    qvec = queries.reshape(token_row_count, KEY_VALUE_HEADS, group, HEAD_WIDTH)
    kmat = keys.reshape(token_row_count, cache_slot_index, KEY_VALUE_HEADS, HEAD_WIDTH)
    value_matrix = value_entries.reshape(
        token_row_count, cache_slot_index, KEY_VALUE_HEADS, HEAD_WIDTH
    )
    own_key = entries[:, 0].reshape(token_row_count, KEY_VALUE_HEADS, HEAD_WIDTH)
    self_value_vector = entries[:, 1].reshape(token_row_count, KEY_VALUE_HEADS, HEAD_WIDTH)
    cache_scores = (
        jnp.einsum("rkgd,rlkd->rkgl", qvec, kmat, preferred_element_type=jnp.float32) * scale
    )
    own_scores = (
        jnp.einsum("rkgd,rkd->rkg", qvec, own_key, preferred_element_type=jnp.float32) * scale
    )
    live = (jnp.arange(cache_slot_index, dtype=jnp.int32)[None, :] < lengths[:, None])[
        :, None, None, :
    ]
    cache_scores = jnp.where(live, cache_scores, -1e30)
    top = jnp.maximum(jnp.max(cache_scores, axis=-1), own_scores)
    cache_p = jnp.where(live, jnp.exp(cache_scores - top[..., None]), 0.0)
    own_p = jnp.exp(own_scores - top)
    total = jnp.sum(cache_p, axis=-1) + own_p
    cache_weight_part = (cache_p / total[..., None]).astype(jnp.bfloat16)
    self_weight_part = (own_p / total).astype(jnp.bfloat16)
    blended_output = jnp.einsum(
        "xtio,xotw->xtiw", cache_weight_part, value_matrix, preferred_element_type=jnp.float32
    )
    blended_output = blended_output + self_weight_part[..., None].astype(
        jnp.float32
    ) * self_value_vector[:, :, None, :].astype(jnp.float32)
    return blended_output.reshape(token_row_count, HEADS * HEAD_WIDTH).astype(jnp.bfloat16)


def prepare(residual, queries, entries, keys, value_entries, lengths, norm_gain):
    attended = attend(queries, entries, keys, value_entries, lengths)
    stream = residual.astype(jnp.float32) + attended.astype(jnp.float32)
    meansq = jnp.mean(stream * stream, axis=-1, keepdims=True)
    normed = (stream / jnp.sqrt(meansq + 1e-06) * norm_gain[None, :]).astype(jnp.bfloat16)
    return (stream, normed)


def combine_table(expert_ids, gate_weights, experts):
    gates = gate_weights / jnp.sum(gate_weights, axis=-1, keepdims=True)
    named = expert_ids[..., None] == jnp.arange(experts, dtype=jnp.int32)
    return jnp.sum(jnp.where(named, gates[..., None], 0.0), axis=-2)


def expert_rows(flat, gate_proj, up_proj, down_proj):
    gate = jnp.dot(flat, gate_proj[0], preferred_element_type=jnp.float32)
    upper = jnp.dot(flat, up_proj[0], preferred_element_type=jnp.float32)
    hidden = (jax.nn.silu(gate) * upper).astype(jnp.bfloat16)
    return jnp.dot(hidden, down_proj[0], preferred_element_type=jnp.float32).astype(jnp.bfloat16)


def on_device(
    residual_in,
    queries,
    new_entries,
    cache_keys,
    cache_values,
    lengths,
    skip_flags,
    expert_ids,
    gate_weights,
    norm_gain,
    gate_proj,
    up_proj,
    down_proj,
):
    micro_count, rows, width = residual_in.shape
    shards = lax.axis_size("ex")
    experts = gate_proj.shape[0] * shards
    table = combine_table(expert_ids, gate_weights, experts)
    mine = lax.all_to_all(table, "ex", split_axis=2, concat_axis=1, tiled=True)
    results = []
    for micro in range(micro_count):
        stream, normed = prepare(
            residual_in[micro],
            queries[micro],
            new_entries[micro],
            cache_keys[micro],
            cache_values[micro],
            lengths[micro],
            norm_gain,
        )
        gathered = lax.all_gather(normed, "ex", axis=0, tiled=True)
        out = expert_rows(gathered, gate_proj, up_proj, down_proj)
        partial = (mine[micro] * out.astype(jnp.float32)).astype(jnp.bfloat16)
        mixture = lax.psum_scatter(partial, "ex", scatter_dimension=0, tiled=True)
        merged = (stream + mixture.astype(jnp.float32)).astype(jnp.bfloat16)
        results.append(
            jnp.where(skip_flags[micro][:, None] == 1, residual_in[micro], merged)
        )
    return jnp.stack(results, axis=0)


def solution(mesh):
    in_specs = (
        P(None, ("groups", "ex"), None),
        P(None, ("groups", "ex"), None),
        P(None, ("groups", "ex"), None, None),
        P(None, ("groups", "ex"), None, None),
        P(None, ("groups", "ex"), None, None),
        P(None, ("groups", "ex")),
        P(None, ("groups", "ex")),
        P(None, ("groups", "ex"), None),
        P(None, ("groups", "ex"), None),
        P(),
        P("ex", None, None),
        P("ex", None, None),
        P("ex", None, None),
    )
    out_specs = P(None, ("groups", "ex"), None)
    return jax.shard_map(
        on_device, mesh=mesh, in_specs=in_specs, out_specs=out_specs, check_vma=False
    )
```

```python
import jax
import jax.numpy as jnp
from jax import lax
from jax.experimental import pallas as pl
from jax.experimental.pallas import tpu as pltpu
from jax.sharding import PartitionSpec as P

HEADS = 16
KEY_VALUE_HEADS = 2
HEAD_WIDTH = 128
ROW_BLOCK = 16


def attend_kernel(len_ref, q_ref, e_ref, k_ref, v_ref, o_ref):
    rows, heads, width = q_ref.shape[1:]
    slots = k_ref.shape[2]
    scale = HEAD_WIDTH ** (-0.5)
    q = q_ref[0]
    entries = e_ref[0]
    group = heads // KEY_VALUE_HEADS
    which = lax.broadcasted_iota(jnp.int32, (rows, heads, width), 1) // group
    zero = jnp.zeros_like(q)
    wide = jnp.concatenate(
        [jnp.where(which == g, q, zero) for g in range(KEY_VALUE_HEADS)], axis=-1
    )
    scores = (
        jnp.einsum("rhd,rld->rhl", wide, k_ref[0], preferred_element_type=jnp.float32) * scale
    )
    own = (
        jnp.sum(
            wide.astype(jnp.float32) * entries[:, 0:1, :].astype(jnp.float32),
            axis=-1,
            keepdims=True,
        )
        * scale
    )
    live = lax.broadcasted_iota(jnp.int32, (rows, heads, slots), 2) < len_ref[0]
    scores = jnp.where(live, scores, -1e30)
    top = jnp.maximum(jnp.max(scores, axis=-1, keepdims=True), own)
    p = jnp.where(live, jnp.exp(scores - top), 0.0)
    own_p = jnp.exp(own - top)
    total = jnp.sum(p, axis=-1, keepdims=True) + own_p
    weights = (p / total).astype(jnp.bfloat16)
    own_w = (own_p / total).astype(jnp.bfloat16).astype(jnp.float32)
    out = jnp.einsum("rhl,rld->rhd", weights, v_ref[0], preferred_element_type=jnp.float32)
    out = out + own_w * entries[:, 1:2, :].astype(jnp.float32)
    result = out[..., :width]
    for g in range(1, KEY_VALUE_HEADS):
        result = jnp.where(which == g, out[..., g * width : (g + 1) * width], result)
    o_ref[...] = result.astype(jnp.bfloat16)


def attend(micro, queries, entries, keys, values, lengths):
    rows, slots, kv_width = keys.shape[1:]
    block = ROW_BLOCK if rows % ROW_BLOCK == 0 else rows
    return pl.pallas_call(
        attend_kernel,
        out_shape=jax.ShapeDtypeStruct((rows, HEADS, HEAD_WIDTH), jnp.bfloat16),
        grid=(rows // block,),
        in_specs=[
            pl.BlockSpec((1, block, 1, 1), lambda i: (micro, i, 0, 0)),
            pl.BlockSpec((1, block, HEADS, HEAD_WIDTH), lambda i: (micro, i, 0, 0)),
            pl.BlockSpec((1, block, 2, kv_width), lambda i: (micro, i, 0, 0)),
            pl.BlockSpec((1, block, slots, kv_width), lambda i: (micro, i, 0, 0)),
            pl.BlockSpec((1, block, slots, kv_width), lambda i: (micro, i, 0, 0)),
        ],
        out_specs=pl.BlockSpec((block, HEADS, HEAD_WIDTH), lambda i: (i, 0, 0)),
        compiler_params=pltpu.CompilerParams(vmem_limit_bytes=32 << 20),
        cost_estimate=pl.CostEstimate(
            flops=rows * HEADS * slots * kv_width * 4,
            bytes_accessed=rows * slots * kv_width * 4,
            transcendentals=rows * HEADS * slots,
        ),
    )(lengths, queries, entries, keys, values)


def combine_table(expert_ids, gate_weights, experts):
    gates = gate_weights / jnp.sum(gate_weights, axis=-1, keepdims=True)
    named = expert_ids[..., None] == jnp.arange(experts, dtype=jnp.int32)
    return jnp.sum(jnp.where(named, gates[..., None], 0.0), axis=-2)


def swap(x, bit, shards):
    return lax.ppermute(x, "ex", [(i, i ^ (1 << bit)) for i in range(shards)])


def weighted_rows(flat, weight, gate_proj, up_proj, down_proj):
    gate = jnp.dot(flat, gate_proj[0], preferred_element_type=jnp.float32)
    upper = jnp.dot(flat, up_proj[0], preferred_element_type=jnp.float32)
    hidden = (jax.nn.silu(gate) * upper).astype(jnp.bfloat16)
    out = jnp.dot(hidden, down_proj[0], preferred_element_type=jnp.float32)
    out = out.astype(jnp.bfloat16).astype(jnp.float32)
    return (weight * out).astype(jnp.bfloat16)


def wide_sum(a, b):
    return (a.astype(jnp.float32) + b.astype(jnp.float32)).astype(jnp.bfloat16)


def on_device(
    residual_in,
    queries,
    new_entries,
    cache_keys,
    cache_values,
    lengths,
    skip_flags,
    expert_ids,
    gate_weights,
    norm_gain,
    gate_proj,
    up_proj,
    down_proj,
):
    micro_count, rows, width = residual_in.shape
    shards = lax.axis_size("ex")
    bits = shards.bit_length() - 1
    experts = gate_proj.shape[0] * shards
    table = combine_table(expert_ids, gate_weights, experts)
    mine = lax.all_to_all(table, "ex", split_axis=2, concat_axis=1, tiled=True)
    mine = mine.reshape(micro_count, shards, rows)
    me = lax.axis_index("ex")
    down = list(range(bits - 1, -1, -1))
    other = down[:-3] + [down[-2], down[-3], down[-1]] if bits >= 3 else down
    orders = (down, other)
    half = rows // 2
    queries = queries.reshape(micro_count, rows, HEADS, HEAD_WIDTH)
    lengths = lengths.reshape(micro_count, rows, 1, 1)
    streams = []
    parts = []
    for micro in range(micro_count):
        attended = attend(micro, queries, new_entries, cache_keys, cache_values, lengths)
        stream = residual_in[micro].astype(jnp.float32) + attended.reshape(rows, width).astype(
            jnp.float32
        )
        meansq = jnp.mean(stream * stream, axis=-1, keepdims=True)
        normed = (stream / jnp.sqrt(meansq + 1e-06) * norm_gain[None, :]).astype(jnp.bfloat16)
        streams.append(stream)
        for side, order in enumerate(orders):
            parts.append((micro, side, order, normed[side * half : (side + 1) * half]))
    sums = {}
    for micro, side, order, buf in parts:
        spread = [0]
        for bit in order:
            spread = spread + [k ^ (1 << bit) for k in spread]
        weight = jnp.take(
            mine[micro, :, side * half : (side + 1) * half],
            jnp.bitwise_xor(me, jnp.array(spread, dtype=jnp.int32)),
            axis=0,
        ).reshape(2, -1, 1)
        for bit in order[:-1]:
            buf = jnp.concatenate([buf, swap(buf, bit, shards)], axis=0)
        far = swap(buf, order[-1], shards)
        back = swap(
            weighted_rows(far, weight[1], gate_proj, up_proj, down_proj), order[-1], shards
        )
        acc = wide_sum(weighted_rows(buf, weight[0], gate_proj, up_proj, down_proj), back)
        for bit in order[-2::-1]:
            keep = acc.shape[0] // 2
            acc = wide_sum(acc[:keep], swap(acc[keep:], bit, shards))
        sums[micro, side] = acc
    results = []
    for micro in range(micro_count):
        mixture = jnp.concatenate([sums[micro, 0], sums[micro, 1]], axis=0)
        merged = (streams[micro] + mixture.astype(jnp.float32)).astype(jnp.bfloat16)
        results.append(jnp.where(skip_flags[micro][:, None] == 1, residual_in[micro], merged))
    return jnp.stack(results, axis=0)


def solution(mesh):
    in_specs = (
        P(None, ("groups", "ex"), None),
        P(None, ("groups", "ex"), None),
        P(None, ("groups", "ex"), None, None),
        P(None, ("groups", "ex"), None, None),
        P(None, ("groups", "ex"), None, None),
        P(None, ("groups", "ex")),
        P(None, ("groups", "ex")),
        P(None, ("groups", "ex"), None),
        P(None, ("groups", "ex"), None),
        P(),
        P("ex", None, None),
        P("ex", None, None),
        P("ex", None, None),
    )
    out_specs = P(None, ("groups", "ex"), None)
    return jax.shard_map(
        on_device, mesh=mesh, in_specs=in_specs, out_specs=out_specs, check_vma=False
    )
```

```python
import jax
import jax.numpy as jnp
from jax import lax
from jax.experimental import pallas as pl
from jax.experimental.pallas import tpu as pltpu
from jax.sharding import PartitionSpec as P

HEADS = 16
KEY_VALUE_HEADS = 2
HEAD_WIDTH = 128
ROW_BLOCK = 16


def attend_kernel(len_ref, q_ref, e_ref, k_ref, v_ref, o_ref):
    rows, heads, width = q_ref.shape[1:]
    slots = k_ref.shape[2]
    scale = HEAD_WIDTH ** (-0.5)
    q = q_ref[0]
    entries = e_ref[0]
    group = heads // KEY_VALUE_HEADS
    which = lax.broadcasted_iota(jnp.int32, (rows, heads, width), 1) // group
    zero = jnp.zeros_like(q)
    wide = jnp.concatenate(
        [jnp.where(which == g, q, zero) for g in range(KEY_VALUE_HEADS)], axis=-1
    )
    scores = (
        jnp.einsum("rhd,rld->rhl", wide, k_ref[0], preferred_element_type=jnp.float32) * scale
    )
    own = (
        jnp.sum(
            wide.astype(jnp.float32) * entries[:, 0:1, :].astype(jnp.float32),
            axis=-1,
            keepdims=True,
        )
        * scale
    )
    live = lax.broadcasted_iota(jnp.int32, (rows, heads, slots), 2) < len_ref[0]
    scores = jnp.where(live, scores, -1e30)
    top = jnp.maximum(jnp.max(scores, axis=-1, keepdims=True), own)
    p = jnp.where(live, jnp.exp(scores - top), 0.0)
    own_p = jnp.exp(own - top)
    total = jnp.sum(p, axis=-1, keepdims=True) + own_p
    weights = (p / total).astype(jnp.bfloat16)
    own_w = (own_p / total).astype(jnp.bfloat16).astype(jnp.float32)
    out = jnp.einsum("rhl,rld->rhd", weights, v_ref[0], preferred_element_type=jnp.float32)
    out = out + own_w * entries[:, 1:2, :].astype(jnp.float32)
    result = out[..., :width]
    for g in range(1, KEY_VALUE_HEADS):
        result = jnp.where(which == g, out[..., g * width : (g + 1) * width], result)
    o_ref[...] = result.astype(jnp.bfloat16)


def attend(micro, queries, entries, keys, values, lengths):
    rows, slots, kv_width = keys.shape[1:]
    block = ROW_BLOCK if rows % ROW_BLOCK == 0 else rows
    return pl.pallas_call(
        attend_kernel,
        out_shape=jax.ShapeDtypeStruct((rows, HEADS, HEAD_WIDTH), jnp.bfloat16),
        grid=(rows // block,),
        in_specs=[
            pl.BlockSpec((1, block, 1, 1), lambda i: (micro, i, 0, 0)),
            pl.BlockSpec((1, block, HEADS, HEAD_WIDTH), lambda i: (micro, i, 0, 0)),
            pl.BlockSpec((1, block, 2, kv_width), lambda i: (micro, i, 0, 0)),
            pl.BlockSpec((1, block, slots, kv_width), lambda i: (micro, i, 0, 0)),
            pl.BlockSpec((1, block, slots, kv_width), lambda i: (micro, i, 0, 0)),
        ],
        out_specs=pl.BlockSpec((block, HEADS, HEAD_WIDTH), lambda i: (i, 0, 0)),
        compiler_params=pltpu.CompilerParams(vmem_limit_bytes=32 << 20),
        cost_estimate=pl.CostEstimate(
            flops=rows * HEADS * slots * kv_width * 4,
            bytes_accessed=rows * slots * kv_width * 4,
            transcendentals=rows * HEADS * slots,
        ),
    )(lengths, queries, entries, keys, values)


def combine_table(expert_ids, gate_weights, experts):
    gates = gate_weights / jnp.sum(gate_weights, axis=-1, keepdims=True)
    named = expert_ids[..., None] == jnp.arange(experts, dtype=jnp.int32)
    return jnp.sum(jnp.where(named, gates[..., None], 0.0), axis=-2)


def swap(x, bit, shards):
    return lax.ppermute(x, "ex", [(i, i ^ (1 << bit)) for i in range(shards)])


def expert_kernel(
    near_ref, far_ref, near_w, far_w, gate_ref, up_ref, down_ref, near_out, far_out, total
):
    step = pl.program_id(0)
    last = pl.num_programs(0) - 1
    for side, x_ref, w_ref, out_ref in ((0, near_ref, near_w, near_out), (1, far_ref, far_w, far_out)):
        x = x_ref[...]
        gate = jnp.dot(x, gate_ref[0], preferred_element_type=jnp.float32)
        upper = jnp.dot(x, up_ref[0], preferred_element_type=jnp.float32)
        hidden = (jax.nn.silu(gate) * upper).astype(jnp.bfloat16)
        part = jnp.dot(hidden, down_ref[0], preferred_element_type=jnp.float32)

        @pl.when(step == 0)
        def _():
            total[side] = part

        @pl.when(step > 0)
        def _():
            total[side] += part

        @pl.when(step == last)
        def _():
            out = total[side].astype(jnp.bfloat16).astype(jnp.float32)
            out_ref[...] = (w_ref[...] * out).astype(jnp.bfloat16)


def weighted_rows(near, far, near_w, far_w, gate_proj, up_proj, down_proj):
    rows, width = near.shape
    hidden = gate_proj.shape[2]
    tile = 256 if hidden % 256 == 0 else hidden
    whole = pl.BlockSpec((rows, width), lambda f: (0, 0))
    column = pl.BlockSpec((rows, 1), lambda f: (0, 0))
    return pl.pallas_call(
        expert_kernel,
        out_shape=[jax.ShapeDtypeStruct((rows, width), jnp.bfloat16)] * 2,
        grid=(hidden // tile,),
        in_specs=[
            whole,
            whole,
            column,
            column,
            pl.BlockSpec((1, width, tile), lambda f: (0, 0, f)),
            pl.BlockSpec((1, width, tile), lambda f: (0, 0, f)),
            pl.BlockSpec((1, tile, width), lambda f: (0, f, 0)),
        ],
        out_specs=[whole, whole],
        scratch_shapes=[pltpu.VMEM((2, rows, width), jnp.float32)],
        compiler_params=pltpu.CompilerParams(vmem_limit_bytes=52 << 20),
        cost_estimate=pl.CostEstimate(
            flops=12 * rows * width * hidden,
            bytes_accessed=6 * width * hidden + 8 * rows * width,
            transcendentals=2 * rows * hidden,
        ),
    )(near, far, near_w, far_w, gate_proj, up_proj, down_proj)


def wide_sum(a, b):
    return (a.astype(jnp.float32) + b.astype(jnp.float32)).astype(jnp.bfloat16)


def on_device(
    residual_in,
    queries,
    new_entries,
    cache_keys,
    cache_values,
    lengths,
    skip_flags,
    expert_ids,
    gate_weights,
    norm_gain,
    gate_proj,
    up_proj,
    down_proj,
):
    micro_count, rows, width = residual_in.shape
    shards = lax.axis_size("ex")
    bits = shards.bit_length() - 1
    experts = gate_proj.shape[0] * shards
    table = combine_table(expert_ids, gate_weights, experts)
    mine = lax.all_to_all(table, "ex", split_axis=2, concat_axis=1, tiled=True)
    mine = mine.reshape(micro_count, shards, rows)
    me = lax.axis_index("ex")
    down = list(range(bits - 1, -1, -1))
    other = down[:-3] + [down[-2], down[-3], down[-1]] if bits >= 3 else down
    orders = (down, other)
    half = rows // 2
    queries = queries.reshape(micro_count, rows, HEADS, HEAD_WIDTH)
    lengths = lengths.reshape(micro_count, rows, 1, 1)
    streams = []
    parts = []
    for micro in range(micro_count):
        attended = attend(micro, queries, new_entries, cache_keys, cache_values, lengths)
        stream = residual_in[micro].astype(jnp.float32) + attended.reshape(rows, width).astype(
            jnp.float32
        )
        meansq = jnp.mean(stream * stream, axis=-1, keepdims=True)
        normed = (stream / jnp.sqrt(meansq + 1e-06) * norm_gain[None, :]).astype(jnp.bfloat16)
        streams.append(stream)
        for side, order in enumerate(orders):
            parts.append((micro, side, order, normed[side * half : (side + 1) * half]))
    sums = {}
    for micro, side, order, buf in parts:
        spread = [0]
        for bit in order:
            spread = spread + [k ^ (1 << bit) for k in spread]
        weight = jnp.take(
            mine[micro, :, side * half : (side + 1) * half],
            jnp.bitwise_xor(me, jnp.array(spread, dtype=jnp.int32)),
            axis=0,
        ).reshape(2, -1, 1)
        for bit in order[:-1]:
            buf = jnp.concatenate([buf, swap(buf, bit, shards)], axis=0)
        far = swap(buf, order[-1], shards)
        near_out, far_out = weighted_rows(
            buf, far, weight[0], weight[1], gate_proj, up_proj, down_proj
        )
        acc = wide_sum(near_out, swap(far_out, order[-1], shards))
        for bit in order[-2::-1]:
            keep = acc.shape[0] // 2
            acc = wide_sum(acc[:keep], swap(acc[keep:], bit, shards))
        sums[micro, side] = acc
    results = []
    for micro in range(micro_count):
        mixture = jnp.concatenate([sums[micro, 0], sums[micro, 1]], axis=0)
        merged = (streams[micro] + mixture.astype(jnp.float32)).astype(jnp.bfloat16)
        results.append(jnp.where(skip_flags[micro][:, None] == 1, residual_in[micro], merged))
    return jnp.stack(results, axis=0)


def solution(mesh):
    in_specs = (
        P(None, ("groups", "ex"), None),
        P(None, ("groups", "ex"), None),
        P(None, ("groups", "ex"), None, None),
        P(None, ("groups", "ex"), None, None),
        P(None, ("groups", "ex"), None, None),
        P(None, ("groups", "ex")),
        P(None, ("groups", "ex")),
        P(None, ("groups", "ex"), None),
        P(None, ("groups", "ex"), None),
        P(),
        P("ex", None, None),
        P("ex", None, None),
        P("ex", None, None),
    )
    out_specs = P(None, ("groups", "ex"), None)
    return jax.shard_map(
        on_device, mesh=mesh, in_specs=in_specs, out_specs=out_specs, check_vma=False
    )
```

```python
import jax
import jax.numpy as jnp
from jax import lax
from jax.experimental import pallas as pl
from jax.experimental.pallas import tpu as pltpu
from jax.sharding import PartitionSpec as P

HEADS = 16
KEY_VALUE_HEADS = 2
HEAD_WIDTH = 128
ROW_BLOCK = 16


def attend_kernel(len_ref, q_ref, e_ref, k_ref, v_ref, o_ref):
    rows, heads, width = q_ref.shape[1:]
    slots = k_ref.shape[2]
    scale = HEAD_WIDTH ** (-0.5)
    q = q_ref[0]
    entries = e_ref[0]
    group = heads // KEY_VALUE_HEADS
    which = lax.broadcasted_iota(jnp.int32, (rows, heads, width), 1) // group
    zero = jnp.zeros_like(q)
    wide = jnp.concatenate(
        [jnp.where(which == g, q, zero) for g in range(KEY_VALUE_HEADS)], axis=-1
    )
    scores = (
        jnp.einsum("rhd,rld->rhl", wide, k_ref[0], preferred_element_type=jnp.float32) * scale
    )
    own = (
        jnp.sum(
            wide.astype(jnp.float32) * entries[:, 0:1, :].astype(jnp.float32),
            axis=-1,
            keepdims=True,
        )
        * scale
    )
    live = lax.broadcasted_iota(jnp.int32, (rows, heads, slots), 2) < len_ref[0]
    scores = jnp.where(live, scores, -1e30)
    top = jnp.maximum(jnp.max(scores, axis=-1, keepdims=True), own)
    p = jnp.where(live, jnp.exp(scores - top), 0.0)
    own_p = jnp.exp(own - top)
    total = jnp.sum(p, axis=-1, keepdims=True) + own_p
    weights = (p / total).astype(jnp.bfloat16)
    own_w = (own_p / total).astype(jnp.bfloat16).astype(jnp.float32)
    out = jnp.einsum("rhl,rld->rhd", weights, v_ref[0], preferred_element_type=jnp.float32)
    out = out + own_w * entries[:, 1:2, :].astype(jnp.float32)
    result = out[..., :width]
    for g in range(1, KEY_VALUE_HEADS):
        result = jnp.where(which == g, out[..., g * width : (g + 1) * width], result)
    o_ref[...] = result.astype(jnp.bfloat16)


def attend(micro, queries, entries, keys, values, lengths):
    rows, slots, kv_width = keys.shape[1:]
    block = ROW_BLOCK if rows % ROW_BLOCK == 0 else rows
    return pl.pallas_call(
        attend_kernel,
        out_shape=jax.ShapeDtypeStruct((rows, HEADS, HEAD_WIDTH), jnp.bfloat16),
        grid=(rows // block,),
        in_specs=[
            pl.BlockSpec((1, block, 1, 1), lambda i: (micro, i, 0, 0)),
            pl.BlockSpec((1, block, HEADS, HEAD_WIDTH), lambda i: (micro, i, 0, 0)),
            pl.BlockSpec((1, block, 2, kv_width), lambda i: (micro, i, 0, 0)),
            pl.BlockSpec((1, block, slots, kv_width), lambda i: (micro, i, 0, 0)),
            pl.BlockSpec((1, block, slots, kv_width), lambda i: (micro, i, 0, 0)),
        ],
        out_specs=pl.BlockSpec((block, HEADS, HEAD_WIDTH), lambda i: (i, 0, 0)),
        compiler_params=pltpu.CompilerParams(vmem_limit_bytes=32 << 20),
        cost_estimate=pl.CostEstimate(
            flops=rows * HEADS * slots * kv_width * 4,
            bytes_accessed=rows * slots * kv_width * 4,
            transcendentals=rows * HEADS * slots,
        ),
    )(lengths, queries, entries, keys, values)


def combine_table(expert_ids, gate_weights, experts):
    gates = gate_weights / jnp.sum(gate_weights, axis=-1, keepdims=True)
    named = expert_ids[..., None] == jnp.arange(experts, dtype=jnp.int32)
    return jnp.sum(jnp.where(named, gates[..., None], 0.0), axis=-2)


def swap(x, bit, shards):
    return lax.ppermute(x, "ex", [(i, i ^ (1 << bit)) for i in range(shards)])


def expert_kernel(
    near_ref, far_ref, near_w, far_w, gate_ref, up_ref, down_ref, near_out, far_out, total
):
    step = pl.program_id(0)
    last = pl.num_programs(0) - 1
    for side, x_ref, w_ref, out_ref in ((0, near_ref, near_w, near_out), (1, far_ref, far_w, far_out)):
        x = x_ref[...]
        gate = jnp.dot(x, gate_ref[0], preferred_element_type=jnp.float32)
        upper = jnp.dot(x, up_ref[0], preferred_element_type=jnp.float32)
        hidden = (jax.nn.silu(gate) * upper).astype(jnp.bfloat16)
        part = jnp.dot(hidden, down_ref[0], preferred_element_type=jnp.float32)

        @pl.when(step == 0)
        def _():
            total[side] = part

        @pl.when(step > 0)
        def _():
            total[side] += part

        @pl.when(step == last)
        def _():
            out = total[side].astype(jnp.bfloat16).astype(jnp.float32)
            out_ref[...] = (w_ref[...] * out).astype(jnp.bfloat16)


def weighted_rows(near, far, near_w, far_w, gate_proj, up_proj, down_proj):
    rows, width = near.shape
    hidden = gate_proj.shape[2]
    tile = 256 if hidden % 256 == 0 else hidden
    whole = pl.BlockSpec((rows, width), lambda f: (0, 0))
    column = pl.BlockSpec((rows, 1), lambda f: (0, 0))
    return pl.pallas_call(
        expert_kernel,
        out_shape=[jax.ShapeDtypeStruct((rows, width), jnp.bfloat16)] * 2,
        grid=(hidden // tile,),
        in_specs=[
            whole,
            whole,
            column,
            column,
            pl.BlockSpec((1, width, tile), lambda f: (0, 0, f)),
            pl.BlockSpec((1, width, tile), lambda f: (0, 0, f)),
            pl.BlockSpec((1, tile, width), lambda f: (0, f, 0)),
        ],
        out_specs=[whole, whole],
        scratch_shapes=[pltpu.VMEM((2, rows, width), jnp.float32)],
        compiler_params=pltpu.CompilerParams(vmem_limit_bytes=52 << 20),
        cost_estimate=pl.CostEstimate(
            flops=12 * rows * width * hidden,
            bytes_accessed=6 * width * hidden + 8 * rows * width,
            transcendentals=2 * rows * hidden,
        ),
    )(near, far, near_w, far_w, gate_proj, up_proj, down_proj)


def wide_sum(a, b):
    return (a.astype(jnp.float32) + b.astype(jnp.float32)).astype(jnp.bfloat16)


def on_device(
    residual_in,
    queries,
    new_entries,
    cache_keys,
    cache_values,
    lengths,
    skip_flags,
    expert_ids,
    gate_weights,
    norm_gain,
    gate_proj,
    up_proj,
    down_proj,
):
    micro_count, rows, width = residual_in.shape
    shards = lax.axis_size("ex")
    bits = shards.bit_length() - 1
    experts = gate_proj.shape[0] * shards
    table = combine_table(expert_ids, gate_weights, experts)
    mine = lax.all_to_all(table, "ex", split_axis=2, concat_axis=1, tiled=True)
    mine = mine.reshape(micro_count, shards, rows)
    me = lax.axis_index("ex")
    down = list(range(bits - 1, -1, -1))
    other = down[:-3] + [down[-2], down[-3], down[-1]] if bits >= 3 else down
    orders = (down, other)
    half = rows // 2
    queries = queries.reshape(micro_count, rows, HEADS, HEAD_WIDTH)
    lengths = lengths.reshape(micro_count, rows, 1, 1)
    streams = []
    parts = []
    for micro in range(micro_count):
        attended = attend(micro, queries, new_entries, cache_keys, cache_values, lengths)
        stream = residual_in[micro].astype(jnp.float32) + attended.reshape(rows, width).astype(
            jnp.float32
        )
        meansq = jnp.mean(stream * stream, axis=-1, keepdims=True)
        normed = (stream / jnp.sqrt(meansq + 1e-06) * norm_gain[None, :]).astype(jnp.bfloat16)
        streams.append(stream)
        for side, order in enumerate(orders):
            parts.append((micro, side, order, normed[side * half : (side + 1) * half]))
    outs = {}
    marks = []
    for micro in range(micro_count):
        sides = [part for part in parts if part[0] == micro]
        bufs = [part[3] for part in sides]
        fars = [None, None]
        for step in range(bits):
            behind = step - max(bits - 3, 0)
            for _, side, order, _ in sides:
                buf = bufs[side]
                if micro > 0 and behind >= 0:
                    buf = lax.optimization_barrier((buf, *marks[min(behind, 2)]))[0]
                got = swap(buf, order[step], shards)
                if step == bits - 1:
                    bufs[side], fars[side] = buf, got
                else:
                    bufs[side] = jnp.concatenate([buf, got], axis=0)
        marks = [tuple(fars)]
        for _, side, order, _ in sides:
            spread = [0]
            for bit in order:
                spread = spread + [k ^ (1 << bit) for k in spread]
            weight = jnp.take(
                mine[micro, :, side * half : (side + 1) * half],
                jnp.bitwise_xor(me, jnp.array(spread, dtype=jnp.int32)),
                axis=0,
            ).reshape(2, -1, 1)
            outs[micro, side] = weighted_rows(
                bufs[side], fars[side], weight[0], weight[1], gate_proj, up_proj, down_proj
            )
            marks.append((outs[micro, side][0],))
    sums = {}
    for micro, side, order, _ in parts:
        near_out, far_out = outs[micro, side]
        acc = wide_sum(near_out, swap(far_out, order[-1], shards))
        for bit in order[-2::-1]:
            keep = acc.shape[0] // 2
            acc = wide_sum(acc[:keep], swap(acc[keep:], bit, shards))
        sums[micro, side] = acc
    results = []
    for micro in range(micro_count):
        mixture = jnp.concatenate([sums[micro, 0], sums[micro, 1]], axis=0)
        merged = (streams[micro] + mixture.astype(jnp.float32)).astype(jnp.bfloat16)
        results.append(jnp.where(skip_flags[micro][:, None] == 1, residual_in[micro], merged))
    return jnp.stack(results, axis=0)


def solution(mesh):
    in_specs = (
        P(None, ("groups", "ex"), None),
        P(None, ("groups", "ex"), None),
        P(None, ("groups", "ex"), None, None),
        P(None, ("groups", "ex"), None, None),
        P(None, ("groups", "ex"), None, None),
        P(None, ("groups", "ex")),
        P(None, ("groups", "ex")),
        P(None, ("groups", "ex"), None),
        P(None, ("groups", "ex"), None),
        P(),
        P("ex", None, None),
        P("ex", None, None),
        P("ex", None, None),
    )
    out_specs = P(None, ("groups", "ex"), None)
    return jax.shard_map(
        on_device, mesh=mesh, in_specs=in_specs, out_specs=out_specs, check_vma=False
    )
```
